32 devices in a mesh: blk: 16 (over z, x, core), rep: 2 (over y).
Axes of the slice: x: 2, y: 2, z: 4, core: 2. Of those that a mesh axis runs over, the one named last changes fastest.
Arguments:
- observed: bfloat16 [128, 64, 4096], P(('blk', 'rep')), may hold values from -6 to 6
- coords: int32 [128, 3], P('blk'), may hold values from 0 to 15
- valid: int32 [128], P('blk'), may hold values from 0 to 1, as said below
- row_owner: int32 [2, 16], replicated, may hold values from 0 to 15, each once within a row
- core: bfloat16 [16384, 128], replicated, may hold values from -6 to 6
- factors: bfloat16 [1024, 3, 128], P('blk'), may hold values from -0.5 to 0.5
Outputs:
- tangent: float32 [1024, 3, 128], P(('blk', 'rep'))
- core_grad: float32 [16384, 128], P(('blk', 'rep'))
The draws below stay inside these ranges and needn't reach their ends.
Inputs may be any that keep to these rules, and one draw needn't show every extreme that they name: `valid`: within each aligned run of 4 entries (the slots of one device) the ones come first; every run has at least one, and some run is all ones.
All inputs are finite; a program needn't handle non-finite values.
Results may differ from the reference program's by a relative error of at most 0.0025.
Values may be sent and summed in bfloat16 or wider, within the bound.
A program may use at most 192 MiB of HBM per device.

```python
import math
import jax
import jax.numpy as jnp
from jax import lax

BS = 64
R = 128
NB_DEV = 4
RBT = 16
MODE = 1024
BLOCKS = 128


def draw_valid(key, part):
    groups = BLOCKS // NB_DEV
    first_key = jax.random.fold_in(key, 11)
    second_key = jax.random.fold_in(key, 23)
    counts = jax.random.randint(first_key, (groups,), 1, NB_DEV + 1)
    chosen = jax.random.randint(second_key, (), 0, groups)
    counts = jnp.where(jnp.arange(groups) == chosen, NB_DEV, counts)
    slots = jnp.arange(NB_DEV)
    return (slots[None, :] < counts[:, None]).astype(jnp.int32).reshape(BLOCKS)


def touch_ends(result, stream_key, low, top_value):
    spot = [jax.random.randint(jax.random.fold_in(stream_key, axis), (), 0, length) for axis, length in enumerate(result.shape)]
    longest = result.shape.index(max(result.shape))
    next_to = spot[:longest] + [(spot[longest] + 1) % result.shape[longest]] + spot[longest + 1:]
    return result.at[tuple(spot)].set(low).at[tuple(next_to)].set(top_value)


def level_of(stream_key, extent, pieces, smallest, top_value):
    level, own = 1.0, jax.random.fold_in(stream_key, 6)
    for position, shards_of in pieces:
        heights = jnp.exp(jax.random.uniform(jax.random.fold_in(own, position), (shards_of,), jnp.float32, smallest / len(pieces), top_value / len(pieces)))
        level = level * jnp.repeat(heights, extent[position] // shards_of).reshape([-1 if axis == position else 1 for axis in range(len(extent))])
    return level


def noise(key, extent, scale, most, cuts=(), kind=jnp.bfloat16):
    drawn = jax.random.normal(key, extent, jnp.float32) * scale
    if len(cuts) > 0:
        drawn = level_of(key, extent, cuts, -0.22, 0.18) * drawn
    return jnp.clip(drawn, min=-most, max=most).astype(kind)


def setup_inputs(seed: int = 0) -> dict:
    splits = jax.random.split(jax.random.key(seed), 7)
    observed = noise(splits[0], (BLOCKS, BS, BS * BS), 1.0, 6.0, ((0, 32),))
    coords = touch_ends(jax.random.randint(splits[1], (BLOCKS, 3), 0, RBT), jax.random.fold_in(splits[1], 1), 0, RBT - 1).astype(jnp.int32)
    valid = draw_valid(jax.random.fold_in(splits[6], 71), 0)
    row_owner = jax.vmap(lambda own: jax.random.permutation(own, RBT))(jax.random.split(splits[3], 2)).reshape((2, RBT)).astype(jnp.int32)
    core = noise(splits[4], (R * R, R), 1.0, 6.0)
    factors = noise(splits[5], (MODE, 3, R), R ** -0.5, 0.5, ((0, 16),))
    return {"observed": observed, "coords": coords, "valid": valid, "row_owner": row_owner, "core": core, "factors": factors}


FACTOR_SCALE = 0.0078125

def storage_blocks(coords, row_owner):
    width = row_owner.shape[1]
    columns = jnp.arange(width, dtype=jnp.int32)[None, :]
    found = []
    for mode_index in range(2):
        match = row_owner[mode_index][None, :] == coords[:, mode_index][:, None]
        found.append(lax.optimization_barrier(jnp.sum(jnp.where(match, columns, 0), axis=1)).astype(jnp.int32))
    found.append(coords[:, 2].astype(jnp.int32))
    return jnp.stack(found, axis=1)

def block_terms(core, a_rows, b_rows, c_rows, block, weight):
    rank = core.shape[1]
    edge = a_rows.shape[0]
    core_f = core.astype(jnp.float32)
    a_f = a_rows.astype(jnp.float32)
    b_f = b_rows.astype(jnp.float32)
    first = jnp.dot(core, c_rows.T, preferred_element_type=jnp.float32).astype(jnp.bfloat16)
    second = jnp.einsum('pqc,bq->pbc', first.reshape(rank, rank, edge).astype(jnp.float32), b_f).astype(jnp.bfloat16)
    predicted = jnp.dot(a_rows, second.reshape(rank, edge * edge), preferred_element_type=jnp.float32)
    residual = ((predicted - block.astype(jnp.float32)) * weight).astype(jnp.bfloat16)
    along_c = jnp.dot(residual.reshape(edge * edge, edge), c_rows, preferred_element_type=jnp.float32).astype(jnp.bfloat16)
    along_bc = jnp.einsum('abr,bq->aqr', along_c.reshape(edge, edge, rank).astype(jnp.float32), b_f).astype(jnp.bfloat16)
    along_bc = along_bc.reshape(edge, rank * rank)
    core_term = jnp.einsum('ap,ak->pk', a_f, along_bc.astype(jnp.float32))
    grad_a = jnp.einsum('ak,pk->ap', along_bc.astype(jnp.float32), core_f.reshape(rank, rank * rank))
    along_ac = jnp.einsum('ap,ak->pk', a_f, along_c.reshape(edge, edge * rank).astype(jnp.float32)).astype(jnp.bfloat16)
    grad_b = jnp.einsum('pbr,pqr->bq', along_ac.reshape(rank, edge, rank).astype(jnp.float32), core_f.reshape(rank, rank, rank))
    along_a = jnp.einsum('ap,ak->pk', a_f, residual.astype(jnp.float32)).astype(jnp.bfloat16)
    along_ab = jnp.einsum('pbc,bq->pqc', along_a.reshape(rank, edge, edge).astype(jnp.float32), b_f).astype(jnp.bfloat16)
    grad_c = jnp.einsum('kc,kr->cr', along_ab.reshape(rank * rank, edge).astype(jnp.float32), core_f)
    return (core_term.reshape(rank * rank, rank), grad_a, grad_b, grad_c)

def reference(observed, coords, valid, row_owner, core, factors):
    edge = BS
    needed = storage_blocks(coords, row_owner)

    def visit(carry, inputs):
        core_acc, panel_acc = carry
        block, place, flag = inputs
        picked = []
        for mode_index in range(3):
            slab = lax.dynamic_slice_in_dim(factors, (place[mode_index] * edge).astype(jnp.int32), edge, 0)
            picked.append(slab[:, mode_index, :])
        weight = flag.astype(jnp.float32)
        core_term, grad_a, grad_b, grad_c = block_terms(core, picked[0], picked[1], picked[2], block, weight)
        for mode_index, grad_block in enumerate((grad_a, grad_b, grad_c)):
            anchor = ((place[mode_index] * edge).astype(jnp.int32), jnp.int32(mode_index), jnp.int32(0))
            current = lax.dynamic_slice(panel_acc, anchor, (edge, 1, R))
            panel_acc = lax.dynamic_update_slice(panel_acc, current + grad_block[:, None, :], anchor)
        return ((core_acc + core_term, panel_acc), None)
    start_core = jnp.zeros((R * R, R), jnp.float32)
    start_panel = jnp.zeros((MODE, 3, R), jnp.float32)
    (core_acc, panel_acc), _ = lax.scan(visit, (start_core, start_panel), (observed, needed, valid))
    grad = panel_acc * FACTOR_SCALE
    core_grad = core_acc * (2.0 / math.sqrt(BLOCKS))
    factor_f = factors.astype(jnp.float32)
    basis = jnp.einsum('smp,smq->mpq', factor_f, grad, precision=lax.Precision.HIGHEST)
    moved = jnp.einsum('smp,mpq->smq', factor_f, basis, precision=lax.Precision.HIGHEST)
    tangent = grad - R / MODE * moved
    return (tangent, core_grad)
```

```python
import math

import jax
import jax.numpy as jnp
from jax import lax
from jax.sharding import PartitionSpec as P

FACTOR_SCALE = 0.0078125


def storage_blocks(coords, row_owner):
    width = row_owner.shape[1]
    columns = jnp.arange(width, dtype=jnp.int32)[None, :]
    found = []
    for mode_index in range(2):
        match = row_owner[mode_index][None, :] == coords[:, mode_index][:, None]
        found.append(jnp.sum(jnp.where(match, columns, 0), axis=1))
    found.append(coords[:, 2])
    return jnp.stack(found, axis=1)


def contract_first(left, right):
    return lax.dot_general(
        left, right, (((0,), (0,)), ((), ())), preferred_element_type=jnp.float32
    )


def contract_last(left, right):
    return lax.dot_general(
        left, right, (((1,), (1,)), ((), ())), preferred_element_type=jnp.float32
    )


def block_terms(core, a_rows, b_rows, c_rows, block, weight):
    rank = core.shape[1]
    edge = a_rows.shape[0]
    first = contract_last(core, c_rows).astype(jnp.bfloat16)
    second = jnp.einsum(
        "pqc,bq->pbc", first.reshape(rank, rank, edge), b_rows, preferred_element_type=jnp.float32
    ).astype(jnp.bfloat16)
    predicted = jnp.dot(
        a_rows, second.reshape(rank, edge * edge), preferred_element_type=jnp.float32
    )
    residual = ((predicted - block.astype(jnp.float32)) * weight).astype(jnp.bfloat16)
    along_c = jnp.dot(
        residual.reshape(edge * edge, edge), c_rows, preferred_element_type=jnp.float32
    ).astype(jnp.bfloat16)
    along_bc = jnp.einsum(
        "abr,bq->aqr", along_c.reshape(edge, edge, rank), b_rows, preferred_element_type=jnp.float32
    ).astype(jnp.bfloat16)
    along_bc = along_bc.reshape(edge, rank * rank)
    grad_a = contract_last(along_bc, core.reshape(rank, rank * rank))
    along_ac = contract_first(a_rows, along_c.reshape(edge, edge * rank)).astype(jnp.bfloat16)
    grad_b = jnp.einsum(
        "pbr,pqr->bq",
        along_ac.reshape(rank, edge, rank),
        core.reshape(rank, rank, rank),
        preferred_element_type=jnp.float32,
    )
    along_a = contract_first(a_rows, residual).astype(jnp.bfloat16)
    along_ab = jnp.einsum(
        "pbc,bq->pqc", along_a.reshape(rank, edge, edge), b_rows, preferred_element_type=jnp.float32
    ).astype(jnp.bfloat16)
    grad_c = contract_first(along_ab.reshape(rank * rank, edge), core)
    return along_bc, jnp.stack([grad_a, grad_b, grad_c])


def bits_of(count):
    return count.bit_length() - 1


def swap(value, axis_name, bit):
    count = lax.axis_size(axis_name)
    return lax.ppermute(value, axis_name, [(i, i ^ (1 << bit)) for i in range(count)])


def own_bit(axis_name, bit):
    return (lax.axis_index(axis_name) >> bit) & 1


def gather_rows(value):
    for step, bit in enumerate(reversed(range(bits_of(lax.axis_size("blk"))))):
        other = swap(value, "blk", bit)
        mine_low = own_bit("blk", bit) == 0
        low = jnp.where(mine_low, value, other)
        high = jnp.where(mine_low, other, value)
        value = jnp.stack([low, high], axis=step)
    return value


def scatter_sum(value, order):
    blk_bits = bits_of(lax.axis_size("blk"))
    total_bits = blk_bits + bits_of(lax.axis_size("rep"))
    value = value.reshape((2,) * total_bits + value.shape[1:])
    left = [("blk", bit) for bit in reversed(range(blk_bits))]
    left += [("rep", bit) for bit in reversed(range(total_bits - blk_bits))]
    for axis_name, bit, kind in order:
        position = left.index((axis_name, bit))
        left.pop(position)
        mine = own_bit(axis_name, bit)
        keep = lax.dynamic_index_in_dim(value, mine, position, keepdims=False)
        send = lax.dynamic_index_in_dim(value, 1 - mine, position, keepdims=False)
        got = swap(send.astype(kind), axis_name, bit)
        value = keep.astype(jnp.float32) + got.astype(jnp.float32)
    return value


def gather_all(value):
    for bit in range(bits_of(lax.axis_size("rep"))):
        other = swap(value, "rep", bit)
        mine_low = own_bit("rep", bit) == 0
        value = jnp.concatenate(
            [jnp.where(mine_low, value, other), jnp.where(mine_low, other, value)], axis=0
        )
    for bit in range(bits_of(lax.axis_size("blk"))):
        other = swap(value, "blk", bit)
        mine_low = own_bit("blk", bit) == 0
        value = jnp.concatenate(
            [jnp.where(mine_low, value, other), jnp.where(mine_low, other, value)], axis=0
        )
    return value


def shards(observed, coords, valid, row_owner, core, factors):
    rep_index = lax.axis_index("rep")
    rep_count = lax.axis_size("rep")
    blk_count = lax.axis_size("blk")
    devices = rep_count * blk_count
    slot_count = observed.shape[0]
    edge = observed.shape[1]
    rank = core.shape[1]
    local_rows = factors.shape[0]
    whole_rows = local_rows * blk_count
    total_blocks = coords.shape[0] * blk_count
    own_rows = local_rows // rep_count
    slot_coords = lax.dynamic_slice_in_dim(coords, rep_index * slot_count, slot_count, 0)
    own_valid = lax.dynamic_slice_in_dim(valid, rep_index * slot_count, slot_count, 0)
    weights = own_valid.astype(jnp.float32)
    needed = storage_blocks(slot_coords, row_owner)
    by_mode = jnp.swapaxes(factors, 0, 1)
    gathered = gather_rows(by_mode).reshape(blk_count, 3, local_rows, rank)
    picked = []
    for mode_index in range(3):
        table = gathered[:, mode_index].reshape(whole_rows // edge, edge, rank)
        picked.append(jnp.take(table, needed[:, mode_index], axis=0, mode="clip"))
    picked_a, picked_b, picked_c = picked

    def visit(carry, inputs):
        a_rows, b_rows, c_rows, block, weight = inputs
        return carry, block_terms(core, a_rows, b_rows, c_rows, block, weight)

    _, (along, grads) = lax.scan(
        visit, 0, (picked_a, picked_b, picked_c, observed, weights)
    )
    core_acc = contract_first(
        picked_a.reshape(slot_count * edge, rank), along.reshape(slot_count * edge, rank * rank)
    )
    picked_f = jnp.stack(picked).astype(jnp.float32)
    basis_part = jnp.einsum("mtsp,tmsq->mpq", picked_f, grads, precision=lax.Precision.HIGHEST)
    panel = jnp.zeros((whole_rows // edge, 3, edge, rank), jnp.float32)
    for slot in range(slot_count):
        for mode_index in range(3):
            anchor = (needed[slot, mode_index], jnp.int32(mode_index), jnp.int32(0), jnp.int32(0))
            current = lax.dynamic_slice(panel, anchor, (1, 1, edge, rank))
            panel = lax.dynamic_update_slice(
                panel, current + grads[slot, mode_index][None, None], anchor
            )

    rep_bits = bits_of(rep_count)
    blk_bits = bits_of(blk_count)
    f32, bf16 = jnp.float32, jnp.bfloat16
    far = [("blk", bit, f32) for bit in range(2, blk_bits)]
    far += [("rep", bit, f32) for bit in range(1, rep_bits)]
    near = [("blk", 0, f32)]
    rep_first = near + [("rep", 0, bf16), ("blk", 1, bf16)] + far
    blk_first = near + [("blk", 1, bf16), ("rep", 0, bf16)] + far

    chunk = rank * rank // devices
    core_chunks = core_acc.reshape(devices, chunk, rank)
    core_low = scatter_sum(core_chunks[:, : chunk // 2], rep_first)
    core_high = scatter_sum(core_chunks[:, chunk // 2 :], blk_first)
    core_sum = jnp.concatenate([core_low, core_high], axis=0)
    core_grad = core_sum * (2.0 / math.sqrt(total_blocks))

    panel_rows = panel.reshape(
        blk_count, local_rows // edge, 3, rep_count, edge // rep_count, rank
    )
    panel_rows = jnp.transpose(panel_rows, (0, 3, 2, 1, 4, 5)).reshape(
        devices, 3 * own_rows, rank
    )
    basis_rows = basis_part.reshape(3 * rank, rank)
    padded = -(-3 * rank // devices) * devices
    basis_rows = jnp.pad(basis_rows, ((0, padded - 3 * rank), (0, 0)))
    small = jnp.concatenate([panel_rows, basis_rows.reshape(devices, -1, rank)], axis=1)
    small_sum = scatter_sum(small, rep_first)
    grad = small_sum[: 3 * own_rows].reshape(3, own_rows, rank) * FACTOR_SCALE
    basis = gather_all(small_sum[3 * own_rows :])[: 3 * rank].reshape(3, rank, rank)
    basis = basis * FACTOR_SCALE
    own_factors = lax.dynamic_slice_in_dim(by_mode, rep_index * own_rows, own_rows, 1).astype(
        jnp.float32
    )
    moved = jnp.einsum("msp,mpq->msq", own_factors, basis, precision=lax.Precision.HIGHEST)
    tangent = grad - rank / whole_rows * moved
    return (jnp.swapaxes(tangent, 0, 1), core_grad)


def solution(mesh):
    in_specs = (
        P(("blk", "rep"), None, None),
        P("blk", None),
        P("blk"),
        P(),
        P(),
        P("blk", None, None),
    )
    out_specs = (P(("blk", "rep"), None, None), P(("blk", "rep"), None))
    return jax.shard_map(shards, mesh=mesh, in_specs=in_specs, out_specs=out_specs, check_vma=False)
```
